32 devices in a mesh: gossip: 16 (over z, x, core), fsdp: 2 (over y).
Axes of the slice: x: 2, y: 2, z: 4, core: 2. Of those that a mesh axis runs over, the one named last changes fastest.
Arguments:
- params: bfloat16 [16, 2560, 2560], P('gossip', 'fsdp'), may hold values from -6 to 6
- activations: bfloat16 [16, 256, 2560], P('gossip', 'fsdp'), may hold values from -36 to 36
- cotangent: bfloat16 [16, 2560, 256], P('gossip', None, 'fsdp'), may hold values from -6 to 6
- push_weight: float32 [16], P('gossip'), may hold values from 0.5 to 2
- gossip_step: int32 [1], replicated, may hold values from 0 to 1048575
Outputs:
- params_next: bfloat16 [16, 2560, 2560], P('gossip', 'fsdp')
- weight_next: float32 [16], P('gossip')
The draws below stay inside these ranges and needn't reach their ends.
Inputs may be any that keep to these rules, and one draw needn't show every extreme that they name: `gossip_step`: the same iteration for all replicas.
All inputs are finite; a program needn't handle non-finite values.
Results may differ from the reference program's by a relative error of at most 0.0039.
Values may be sent and summed in bfloat16 or wider, within the bound.
A program may use at most 64 MiB of HBM per device.

```python
import math
import jax
import jax.numpy as jnp
from jax import lax

F = 2560
H = 2560
LEVELS = 4
TOKENS = 256
GROUPS = 16


def draw_activations(key, part):
    key_rows, key_cols, key_base = jax.random.split(key, 3)
    row_scale = jnp.exp(jax.random.uniform(key_rows, (GROUPS, TOKENS, 1), jnp.float32, -1.2, 1.1))
    col_scale = jnp.exp(jax.random.uniform(key_cols, (GROUPS, 1, F), jnp.float32, -1.2, 1.1))
    base = jnp.clip(jax.random.normal(key_base, (GROUPS, TOKENS, F), jnp.float32), -4.0, 4.0)
    return (base * row_scale * col_scale).astype(jnp.bfloat16)


def level_of(key, dims, cuts, smallest, top_value):
    level, own = 1.0, jax.random.fold_in(key, 6)
    for axis_at, parts in cuts:
        draws = jnp.exp(jax.random.uniform(jax.random.fold_in(own, axis_at), (parts,), jnp.float32, smallest / len(cuts), top_value / len(cuts)))
        level = level * jnp.repeat(draws, dims[axis_at] // parts).reshape([-1 if axis == axis_at else 1 for axis in range(len(dims))])
    return level


def centred(stream_key, shape, scale, limit, cuts=(), held_as=jnp.bfloat16):
    factor_of = level_of(stream_key, shape, cuts, -0.22, 0.18) if cuts else 1.0
    values = jax.random.normal(stream_key, shape, jnp.float32) * scale * factor_of
    return jnp.minimum(jnp.maximum(values, -limit), limit).astype(held_as)


def setup_inputs(seed: int = 0) -> dict:
    key_list = jax.random.split(jax.random.key(seed), 6)
    params = centred(key_list[0], (GROUPS, H, F), 1.0, 6.0, ((0, 16), (1, 2)))
    activations = draw_activations(jax.random.fold_in(key_list[5], 71), 0)
    cotangent = centred(key_list[2], (GROUPS, H, TOKENS), 1.0, 6.0, ((0, 16), (2, 2)))
    push_weight = jnp.clip(0.5 + 1.5 * jax.random.uniform(key_list[3], (GROUPS,), jnp.float32) ** level_of(key_list[3], (GROUPS,), ((0, 16),), -0.2, 0.2), 0.5, 2.0)
    gossip_step = jax.random.randint(key_list[4], (1,), 0, 1048576).astype(jnp.int32)
    return {"params": params, "activations": activations, "cotangent": cotangent, "push_weight": push_weight, "gossip_step": gossip_step}


EPS = 1e-05
STEP_SIZE = 2.0
DECAY = 0.1

def reference(params, activations, cotangent, push_weight, gossip_step):
    scale = 1.0 / math.sqrt(F)

    def one_group(items):
        weights, tokens, upstream, weight = items
        numer = weights.astype(jnp.float32)
        debiased = (numer / weight).astype(jnp.bfloat16)
        tok_f = tokens.astype(jnp.float32)
        normed = (tok_f * lax.rsqrt(lax.optimization_barrier(jnp.mean(tok_f * tok_f, axis=1, keepdims=True)) + EPS)).astype(jnp.bfloat16)
        grad = jnp.dot(upstream, normed, preferred_element_type=jnp.float32) * scale
        return (numer - STEP_SIZE * (grad + DECAY * debiased.astype(jnp.float32))) * 0.5
    kept = lax.map(one_group, (params, activations, cotangent, push_weight))
    level = jnp.remainder(gossip_step[0].astype(jnp.int32), jnp.int32(LEVELS))
    offset = jnp.left_shift(jnp.int32(1), level)
    message = (params.astype(jnp.float32) * 0.5).astype(jnp.bfloat16)
    received = jnp.roll(message, offset, axis=0)
    params_next = (kept + received.astype(jnp.float32)).astype(jnp.bfloat16)
    half_weight = (push_weight * 0.5).astype(jnp.bfloat16)
    weight_next = push_weight * 0.5 + jnp.roll(half_weight, offset, axis=0).astype(jnp.float32)
    return (params_next, weight_next)
```

```python
from functools import partial
import math

import jax
import jax.numpy as jnp
from jax import lax
from jax.experimental import pallas as pl
from jax.experimental.pallas import tpu as pltpu
from jax.sharding import PartitionSpec as P

LEVELS = 4
EPS = 1e-05
STEP_SIZE = 2.0
DECAY = 0.1
CHUNK = 64
NORM_ROWS = 32
MESH = pl.DeviceIdType.MESH


def kernel(
    level, groups, parts,
    params, tokens, upstream, weight,
    params_next, weight_next,
    numer, received, kept, mixed, act, normed, cot, weight_in,
    push_send, push_recv, out_sem, act_send, act_recv, cot_send, cot_recv, small_sem,
):
    rows, feats = numer.shape
    own_tokens = act.shape[1]
    chunk = math.gcd(rows, CHUNK)
    chunks = rows // chunk
    scale = 1.0 / math.sqrt(feats)
    g, f = lax.axis_index("gossip"), lax.axis_index("fsdp")
    ahead = lax.rem(g + (1 << level), groups)
    behind = lax.rem(g + groups - (1 << level), groups)

    barrier = pltpu.get_barrier_semaphore()
    partners = [(ahead, f), (behind, f)]
    partners += [(g, lax.rem(f + d, parts)) for d in range(1, parts)]
    for partner in partners:
        pl.semaphore_signal(barrier, inc=1, device_id=partner, device_id_type=MESH)
    pl.semaphore_wait(barrier, len(partners))

    def window(c):
        return pl.ds(pl.multiple_of(c * chunk, chunk), chunk)

    def push(c):
        return pltpu.make_async_remote_copy(
            src_ref=params.at[0, window(c)],
            dst_ref=received.at[window(c)],
            send_sem=push_send.at[c],
            recv_sem=push_recv.at[c],
            device_id=(ahead, f),
            device_id_type=MESH,
        )

    def rows_of(part):
        return pl.ds(pl.multiple_of(part * rows, rows), rows)

    def share(d):
        part = lax.rem(f + d, parts)
        return (
            pltpu.make_async_remote_copy(
                src_ref=upstream.at[0, rows_of(part)],
                dst_ref=cot.at[d],
                send_sem=cot_send.at[d],
                recv_sem=cot_recv.at[d],
                device_id=(g, part),
                device_id_type=MESH,
            ),
            pltpu.make_async_remote_copy(
                src_ref=tokens.at[0],
                dst_ref=act.at[d],
                send_sem=act_send.at[d],
                recv_sem=act_recv.at[d],
                device_id=(g, part),
                device_id_type=MESH,
            ),
        )

    @pl.loop(0, chunks)
    def _(c):
        push(c).start()

    for d in range(1, parts):
        for copy in share(d):
            copy.start()
    push_weight = pltpu.make_async_remote_copy(
        src_ref=weight,
        dst_ref=weight_in,
        send_sem=small_sem.at[0],
        recv_sem=small_sem.at[1],
        device_id=(ahead, f),
        device_id_type=MESH,
    )
    push_weight.start()

    own = [
        pltpu.make_async_copy(tokens.at[0], act.at[0], act_recv.at[0]),
        pltpu.make_async_copy(upstream.at[0, rows_of(f)], cot.at[0], cot_recv.at[0]),
        pltpu.make_async_copy(params.at[0], numer, small_sem.at[2]),
    ]
    for copy in own:
        copy.start()
    for copy in own:
        copy.wait()
    for d in range(1, parts):
        for copy in share(d):
            copy.wait()

    block = math.gcd(own_tokens, NORM_ROWS)
    for d in range(parts):

        @pl.loop(0, own_tokens // block)
        def _(t):
            at = pl.ds(pl.multiple_of(t * block, block), block)
            tok = act[d, at, :].astype(jnp.float32)
            mean = jnp.mean(tok * tok, axis=1, keepdims=True)
            normed[d, at, :] = (tok * lax.rsqrt(mean + EPS)).astype(jnp.bfloat16)

    @pl.loop(0, chunks)
    def _(c):
        at = window(c)
        grad = jnp.zeros((chunk, feats), jnp.float32)
        for d in range(parts):
            grad += jnp.dot(cot[d, at, :], normed[d], preferred_element_type=jnp.float32)
        mine = numer[at, :].astype(jnp.float32)
        debiased = (mine / weight[0:1, 0:1]).astype(jnp.bfloat16).astype(jnp.float32)
        kept[at, :] = (mine - STEP_SIZE * (grad * scale + DECAY * debiased)) * 0.5

    push_weight.wait()
    half = (weight_in[...] * 0.5).astype(jnp.bfloat16).astype(jnp.float32)
    weight_next[...] = weight[...] * 0.5 + half

    def put(c):
        return pltpu.make_async_copy(
            mixed.at[window(c)], params_next.at[0, window(c)], out_sem.at[c]
        )

    @pl.loop(0, chunks)
    def _(c):
        at = window(c)
        push(c).wait_recv()
        message = (received[at, :].astype(jnp.float32) * 0.5).astype(jnp.bfloat16)
        mixed[at, :] = (kept[at, :] + message.astype(jnp.float32)).astype(jnp.bfloat16)
        put(c).start()

    @pl.loop(0, chunks)
    def _(c):
        push(c).wait_send()
        put(c).wait()


def mix(level, params, activations, cotangent, weight):
    groups, parts = lax.axis_size("gossip"), lax.axis_size("fsdp")
    _, rows, feats = params.shape
    own_tokens = activations.shape[1]
    chunks = rows // math.gcd(rows, CHUNK)
    anywhere = pl.BlockSpec(memory_space=pl.ANY)
    vector = pl.BlockSpec(memory_space=pltpu.VMEM)
    dma = pltpu.SemaphoreType.DMA
    return pl.pallas_call(
        partial(kernel, level, groups, parts),
        name=f"mix_{level}",
        out_shape=(
            jax.ShapeDtypeStruct(params.shape, jnp.bfloat16),
            jax.ShapeDtypeStruct(weight.shape, jnp.float32),
        ),
        in_specs=[anywhere, anywhere, anywhere, vector],
        out_specs=(anywhere, vector),
        scratch_shapes=[
            pltpu.VMEM((rows, feats), jnp.bfloat16),
            pltpu.VMEM((rows, feats), jnp.bfloat16),
            pltpu.VMEM((rows, feats), jnp.float32),
            pltpu.VMEM((rows, feats), jnp.bfloat16),
            pltpu.VMEM((parts, own_tokens, feats), jnp.bfloat16),
            pltpu.VMEM((parts, own_tokens, feats), jnp.bfloat16),
            pltpu.VMEM((parts, rows, own_tokens), jnp.bfloat16),
            pltpu.VMEM(weight.shape, jnp.float32),
            dma((chunks,)),
            dma((chunks,)),
            dma((chunks,)),
            dma((parts,)),
            dma((parts,)),
            dma((parts,)),
            dma((parts,)),
            dma((3,)),
        ],
        compiler_params=pltpu.CompilerParams(
            collective_id=level, has_side_effects=True, vmem_limit_bytes=56 * 2**20
        ),
    )(params, activations, cotangent, weight)


def shards(params, activations, cotangent, push_weight, gossip_step):
    weight = jnp.broadcast_to(push_weight[:, None], (8, 128))
    chosen = jnp.remainder(gossip_step[0], jnp.int32(LEVELS))
    branches = [partial(mix, level) for level in range(LEVELS)]
    params_next, mixed_weight = lax.switch(
        chosen, branches, params, activations, cotangent, weight
    )
    return params_next, mixed_weight[0, :1]


def solution(mesh):
    placed = (
        P("gossip", "fsdp", None),
        P("gossip", "fsdp", None),
        P("gossip", None, "fsdp"),
        P("gossip"),
        P(),
    )
    return jax.shard_map(
        shards,
        mesh=mesh,
        in_specs=placed,
        out_specs=(P("gossip", "fsdp", None), P("gossip")),
        check_vma=False,
    )
```

```python
from functools import partial
import math

import jax
import jax.numpy as jnp
from jax import lax
from jax.experimental import pallas as pl
from jax.experimental.pallas import tpu as pltpu
from jax.sharding import PartitionSpec as P

LEVELS = 4
EPS = 1e-05
STEP_SIZE = 2.0
DECAY = 0.1
CHUNK = 64
NORM_ROWS = 32
MESH = pl.DeviceIdType.MESH


def kernel(
    level, groups, parts,
    params, tokens, upstream, weight,
    params_next, weight_next,
    numer, received, kept, mixed, act, normed, cot, weight_in,
    push_send, push_recv, out_sem, act_send, act_recv, cot_send, cot_recv, small_sem,
):
    rows, feats = numer.shape
    own_tokens = act.shape[1]
    chunk = math.gcd(rows, CHUNK)
    chunks = rows // chunk
    scale = 1.0 / math.sqrt(feats)
    g, f = lax.axis_index("gossip"), lax.axis_index("fsdp")
    ahead = lax.rem(g + (1 << level), groups)
    behind = lax.rem(g + groups - (1 << level), groups)

    barrier = pltpu.get_barrier_semaphore()
    partners = [(ahead, f), (behind, f)]
    partners += [(g, lax.rem(f + d, parts)) for d in range(1, parts)]
    for partner in partners:
        pl.semaphore_signal(barrier, inc=1, device_id=partner, device_id_type=MESH)
    pl.semaphore_wait(barrier, len(partners))

    def window(c):
        return pl.ds(pl.multiple_of(c * chunk, chunk), chunk)

    def push(c):
        return pltpu.make_async_remote_copy(
            src_ref=params.at[0, window(c)],
            dst_ref=received.at[window(c)],
            send_sem=push_send.at[c],
            recv_sem=push_recv.at[c],
            device_id=(ahead, f),
            device_id_type=MESH,
        )

    def rows_of(part):
        return pl.ds(pl.multiple_of(part * rows, rows), rows)

    def share(d):
        part = lax.rem(f + d, parts)
        return (
            pltpu.make_async_remote_copy(
                src_ref=upstream.at[0, rows_of(part)],
                dst_ref=cot.at[d],
                send_sem=cot_send.at[d],
                recv_sem=cot_recv.at[d],
                device_id=(g, part),
                device_id_type=MESH,
            ),
            pltpu.make_async_remote_copy(
                src_ref=tokens.at[0],
                dst_ref=act.at[d],
                send_sem=act_send.at[d],
                recv_sem=act_recv.at[d],
                device_id=(g, part),
                device_id_type=MESH,
            ),
        )

    for d in range(1, parts):
        for copy in share(d):
            copy.start()
    push_weight = pltpu.make_async_remote_copy(
        src_ref=weight,
        dst_ref=weight_in,
        send_sem=small_sem.at[0],
        recv_sem=small_sem.at[1],
        device_id=(ahead, f),
        device_id_type=MESH,
    )
    push_weight.start()

    @pl.loop(0, chunks)
    def _(c):
        push(c).start()

    own = [
        pltpu.make_async_copy(tokens.at[0], act.at[0], act_recv.at[0]),
        pltpu.make_async_copy(upstream.at[0, rows_of(f)], cot.at[0], cot_recv.at[0]),
        pltpu.make_async_copy(params.at[0], numer, small_sem.at[2]),
    ]
    for copy in own:
        copy.start()
    for copy in own:
        copy.wait()
    for d in range(1, parts):
        for copy in share(d):
            copy.wait()

    block = math.gcd(own_tokens, NORM_ROWS)
    for d in range(parts):

        @pl.loop(0, own_tokens // block)
        def _(t):
            at = pl.ds(pl.multiple_of(t * block, block), block)
            tok = act[d, at, :].astype(jnp.float32)
            mean = jnp.mean(tok * tok, axis=1, keepdims=True)
            normed[d, at, :] = (tok * lax.rsqrt(mean + EPS)).astype(jnp.bfloat16)

    @pl.loop(0, chunks)
    def _(c):
        at = window(c)
        grad = jnp.zeros((chunk, feats), jnp.float32)
        for d in range(parts):
            grad += jnp.dot(cot[d, at, :], normed[d], preferred_element_type=jnp.float32)
        mine = numer[at, :].astype(jnp.float32)
        debiased = (mine / weight[0:1, 0:1]).astype(jnp.bfloat16).astype(jnp.float32)
        kept[at, :] = (mine - STEP_SIZE * (grad * scale + DECAY * debiased)) * 0.5

    push_weight.wait()
    half = (weight_in[...] * 0.5).astype(jnp.bfloat16).astype(jnp.float32)
    weight_next[...] = weight[...] * 0.5 + half

    def put(c):
        return pltpu.make_async_copy(
            mixed.at[window(c)], params_next.at[0, window(c)], out_sem.at[c]
        )

    @pl.loop(0, chunks)
    def _(c):
        at = window(c)
        push(c).wait_recv()
        message = (received[at, :].astype(jnp.float32) * 0.5).astype(jnp.bfloat16)
        mixed[at, :] = (kept[at, :] + message.astype(jnp.float32)).astype(jnp.bfloat16)
        put(c).start()

    @pl.loop(0, chunks)
    def _(c):
        push(c).wait_send()
        put(c).wait()


def mix(level, params, activations, cotangent, weight):
    groups, parts = lax.axis_size("gossip"), lax.axis_size("fsdp")
    _, rows, feats = params.shape
    own_tokens = activations.shape[1]
    chunks = rows // math.gcd(rows, CHUNK)
    anywhere = pl.BlockSpec(memory_space=pl.ANY)
    vector = pl.BlockSpec(memory_space=pltpu.VMEM)
    dma = pltpu.SemaphoreType.DMA
    return pl.pallas_call(
        partial(kernel, level, groups, parts),
        name=f"mix_{level}",
        out_shape=(
            jax.ShapeDtypeStruct(params.shape, jnp.bfloat16),
            jax.ShapeDtypeStruct(weight.shape, jnp.float32),
        ),
        in_specs=[anywhere, anywhere, anywhere, vector],
        out_specs=(anywhere, vector),
        scratch_shapes=[
            pltpu.VMEM((rows, feats), jnp.bfloat16),
            pltpu.VMEM((rows, feats), jnp.bfloat16),
            pltpu.VMEM((rows, feats), jnp.float32),
            pltpu.VMEM((rows, feats), jnp.bfloat16),
            pltpu.VMEM((parts, own_tokens, feats), jnp.bfloat16),
            pltpu.VMEM((parts, own_tokens, feats), jnp.bfloat16),
            pltpu.VMEM((parts, rows, own_tokens), jnp.bfloat16),
            pltpu.VMEM(weight.shape, jnp.float32),
            dma((chunks,)),
            dma((chunks,)),
            dma((chunks,)),
            dma((parts,)),
            dma((parts,)),
            dma((parts,)),
            dma((parts,)),
            dma((3,)),
        ],
        compiler_params=pltpu.CompilerParams(
            collective_id=level, has_side_effects=True, vmem_limit_bytes=56 * 2**20
        ),
    )(params, activations, cotangent, weight)


def shards(params, activations, cotangent, push_weight, gossip_step):
    weight = jnp.broadcast_to(push_weight[:, None], (8, 128))
    chosen = jnp.remainder(gossip_step[0], jnp.int32(LEVELS))
    branches = [partial(mix, level) for level in range(LEVELS)]
    params_next, mixed_weight = lax.switch(
        chosen, branches, params, activations, cotangent, weight
    )
    return params_next, mixed_weight[0, :1]


def solution(mesh):
    placed = (
        P("gossip", "fsdp", None),
        P("gossip", "fsdp", None),
        P("gossip", None, "fsdp"),
        P("gossip"),
        P(),
    )
    return jax.shard_map(
        shards,
        mesh=mesh,
        in_specs=placed,
        out_specs=(P("gossip", "fsdp", None), P("gossip")),
        check_vma=False,
    )
```

```python
from functools import partial
import math

import jax
import jax.numpy as jnp
from jax import lax
from jax.experimental import pallas as pl
from jax.experimental.pallas import tpu as pltpu
from jax.sharding import PartitionSpec as P

LEVELS = 4
EPS = 1e-05
STEP_SIZE = 2.0
DECAY = 0.1
CHUNK = 64
NORM_ROWS = 32
MESH = pl.DeviceIdType.MESH


def kernel(
    level, groups, parts,
    params, tokens, upstream, weight,
    params_next, weight_next,
    numer, received, kept, mixed, act, normed, cot, weight_own, weight_in,
    push_send, push_recv, out_sem, act_send, act_recv, cot_send, cot_recv, small_sem,
):
    rows, feats = numer.shape
    own_tokens = act.shape[1]
    chunk = math.gcd(rows, CHUNK)
    chunks = rows // chunk
    scale = 1.0 / math.sqrt(feats)
    g, f = lax.axis_index("gossip"), lax.axis_index("fsdp")
    ahead = lax.rem(g + (1 << level), groups)
    behind = lax.rem(g + groups - (1 << level), groups)

    barrier = pltpu.get_barrier_semaphore()
    partners = [(behind, f)] + [(g, lax.rem(f + d, parts)) for d in range(1, parts)]
    for partner in partners:
        pl.semaphore_signal(barrier, inc=1, device_id=partner, device_id_type=MESH)
    pl.semaphore_wait(barrier, len(partners))

    def window(c):
        return pl.ds(pl.multiple_of(c * chunk, chunk), chunk)

    def push(c):
        return pltpu.make_async_remote_copy(
            src_ref=params.at[0, window(c)],
            dst_ref=received.at[window(c)],
            send_sem=push_send.at[c],
            recv_sem=push_recv.at[c],
            device_id=(ahead, f),
            device_id_type=MESH,
        )

    def rows_of(part):
        return pl.ds(pl.multiple_of(part * rows, rows), rows)

    def share(d):
        part = lax.rem(f + d, parts)
        return (
            pltpu.make_async_remote_copy(
                src_ref=upstream.at[0, rows_of(part)],
                dst_ref=cot.at[d],
                send_sem=cot_send.at[d],
                recv_sem=cot_recv.at[d],
                device_id=(g, part),
                device_id_type=MESH,
            ),
            pltpu.make_async_remote_copy(
                src_ref=tokens.at[0],
                dst_ref=act.at[d],
                send_sem=act_send.at[d],
                recv_sem=act_recv.at[d],
                device_id=(g, part),
                device_id_type=MESH,
            ),
        )

    for d in range(1, parts):
        for copy in share(d):
            copy.start()
    push_weight = pltpu.make_async_remote_copy(
        src_ref=weight,
        dst_ref=weight_in,
        send_sem=small_sem.at[0],
        recv_sem=small_sem.at[1],
        device_id=(ahead, f),
        device_id_type=MESH,
    )
    push_weight.start()

    @pl.loop(0, chunks)
    def _(c):
        push(c).start()

    own = [
        pltpu.make_async_copy(tokens.at[0], act.at[0], act_recv.at[0]),
        pltpu.make_async_copy(upstream.at[0, rows_of(f)], cot.at[0], cot_recv.at[0]),
        pltpu.make_async_copy(params.at[0], numer, small_sem.at[2]),
        pltpu.make_async_copy(weight, weight_own, small_sem.at[3]),
    ]
    for copy in own:
        copy.start()
    for copy in own:
        copy.wait()
    for d in range(1, parts):
        for copy in share(d):
            copy.wait()

    block = math.gcd(own_tokens, NORM_ROWS)
    for d in range(parts):

        @pl.loop(0, own_tokens // block)
        def _(t):
            at = pl.ds(pl.multiple_of(t * block, block), block)
            tok = act[d, at, :].astype(jnp.float32)
            mean = jnp.mean(tok * tok, axis=1, keepdims=True)
            normed[d, at, :] = (tok * lax.rsqrt(mean + EPS)).astype(jnp.bfloat16)

    @pl.loop(0, chunks)
    def _(c):
        at = window(c)
        grad = jnp.zeros((chunk, feats), jnp.float32)
        for d in range(parts):
            grad += jnp.dot(cot[d, at, :], normed[d], preferred_element_type=jnp.float32)
        mine = numer[at, :].astype(jnp.float32)
        debiased = (mine / weight_own[0]).astype(jnp.bfloat16).astype(jnp.float32)
        kept[at, :] = (mine - STEP_SIZE * (grad * scale + DECAY * debiased)) * 0.5

    push_weight.wait()
    half = (jnp.full(weight_next.shape, weight_in[0]) * 0.5).astype(jnp.bfloat16)
    weight_next[...] = weight_own[0] * 0.5 + half.astype(jnp.float32)

    def put(c):
        return pltpu.make_async_copy(
            mixed.at[window(c)], params_next.at[0, window(c)], out_sem.at[c]
        )

    @pl.loop(0, chunks)
    def _(c):
        at = window(c)
        push(c).wait_recv()
        message = (received[at, :].astype(jnp.float32) * 0.5).astype(jnp.bfloat16)
        mixed[at, :] = (kept[at, :] + message.astype(jnp.float32)).astype(jnp.bfloat16)
        put(c).start()

    @pl.loop(0, chunks)
    def _(c):
        push(c).wait_send()
        put(c).wait()


def mix(level, params, activations, cotangent, weight):
    groups, parts = lax.axis_size("gossip"), lax.axis_size("fsdp")
    _, rows, feats = params.shape
    own_tokens = activations.shape[1]
    chunks = rows // math.gcd(rows, CHUNK)
    anywhere = pl.BlockSpec(memory_space=pl.ANY)
    vector = pl.BlockSpec(memory_space=pltpu.VMEM)
    dma = pltpu.SemaphoreType.DMA
    return pl.pallas_call(
        partial(kernel, level, groups, parts),
        name=f"mix_{level}",
        out_shape=(
            jax.ShapeDtypeStruct(params.shape, jnp.bfloat16),
            jax.ShapeDtypeStruct((8, 128), jnp.float32),
        ),
        in_specs=[anywhere] * 4,
        out_specs=(anywhere, vector),
        scratch_shapes=[
            pltpu.VMEM((rows, feats), jnp.bfloat16),
            pltpu.VMEM((rows, feats), jnp.bfloat16),
            pltpu.VMEM((rows, feats), jnp.float32),
            pltpu.VMEM((rows, feats), jnp.bfloat16),
            pltpu.VMEM((parts, own_tokens, feats), jnp.bfloat16),
            pltpu.VMEM((parts, own_tokens, feats), jnp.bfloat16),
            pltpu.VMEM((parts, rows, own_tokens), jnp.bfloat16),
            pltpu.SMEM(weight.shape, jnp.float32),
            pltpu.SMEM(weight.shape, jnp.float32),
            dma((chunks,)),
            dma((chunks,)),
            dma((chunks,)),
            dma((parts,)),
            dma((parts,)),
            dma((parts,)),
            dma((parts,)),
            dma((4,)),
        ],
        compiler_params=pltpu.CompilerParams(
            collective_id=level, has_side_effects=True, vmem_limit_bytes=56 * 2**20
        ),
    )(params, activations, cotangent, weight)


def shards(params, activations, cotangent, push_weight, gossip_step):
    chosen = jnp.remainder(gossip_step[0], jnp.int32(LEVELS))
    branches = [partial(mix, level) for level in range(LEVELS)]
    params_next, mixed_weight = lax.switch(
        chosen, branches, params, activations, cotangent, push_weight
    )
    return params_next, mixed_weight[0, :1]


def solution(mesh):
    placed = (
        P("gossip", "fsdp", None),
        P("gossip", "fsdp", None),
        P("gossip", None, "fsdp"),
        P("gossip"),
        P(),
    )
    return jax.shard_map(
        shards,
        mesh=mesh,
        in_specs=placed,
        out_specs=(P("gossip", "fsdp", None), P("gossip")),
        check_vma=False,
    )
```
